1024 devices in a mesh: prow: 64 (over z, x), pcol: 16 (over y, core).
Axes of the slice: x: 4, y: 8, z: 16, core: 2. Of those that a mesh axis runs over, the one named last changes fastest.
Arguments:
- slab: float32 [32768, 8192], P('prow', 'pcol'), may hold values from -6 to 6
- panel: float32 [32768, 512], P('prow', 'pcol'), may hold values from -0.25 to 0.25
- tri_inverse: float32 [512, 512], replicated, as said below
- pivots: int32 [512], replicated, may hold values from 512 to 32767, as said below
Outputs:
- updated: float32 [32768, 8192], P('prow', 'pcol')
The draws below stay inside these ranges and needn't reach their ends.
Inputs may be any that keep to these rules, and one draw needn't show every extreme that they name: The pivots are distinct row numbers of the rows below the first 512. At most 10 of them fall among the 512 rows of one device, and some device holds exactly 10. `tri_inverse`: lower triangular with zeros above the diagonal; the diagonal lies between 0.8 and 1.2.
All inputs are finite; a program needn't handle non-finite values.
Results may differ from the reference program's by a relative error of at most 0.000053.
Values sent between devices are 32-bit elements; how exact they have to be, the bound alone decides.
A program may use at most 32 MiB of HBM per device.

```python
import jax
import jax.numpy as jnp
from jax import lax

NB = 512
ROWS = 32768
COLS = 8192
PIV_MOST = 10
N_PROW = 64


def draw_pivots(key, part):
    first, second, third = jax.random.split(jax.random.fold_in(key, 11), 3)
    capacity = PIV_MOST
    slots_all = (N_PROW - 1) * capacity
    spare = jax.random.permutation(first, slots_all - 1 - capacity)[:NB - capacity - 1] + capacity
    chosen = jnp.concatenate([jnp.arange(capacity, dtype=jnp.int32), spare.astype(jnp.int32), jnp.array([slots_all - 1], jnp.int32)])
    device_row = 1 + chosen // capacity
    band = chosen % capacity
    spacing = NB // capacity
    offset = jax.random.randint(second, (NB,), 0, spacing).astype(jnp.int32)
    offset = offset.at[0].set(0)
    local_row = band * spacing + offset
    local_row = local_row.at[NB - 1].set(NB - 1)
    values = (device_row * NB + local_row).astype(jnp.int32)
    order = jax.random.permutation(third, NB)
    return values[order].astype(jnp.int32)


def draw_tri_inverse(key, part):
    first, second = jax.random.split(jax.random.fold_in(key, 23))
    lower = 0.7 * jax.random.normal(first, (NB, NB), jnp.float32) / jnp.sqrt(NB * 1.0)
    diag_vals = jax.random.uniform(second, (NB,), jnp.float32, 0.8, 1.2)
    return jnp.tril(lower, -1) + jnp.diag(diag_vals)


def block_levels(stream_key, extent, cuts, least, high):
    def one(dim, parts):
        draws = jax.random.uniform(jax.random.fold_in(jax.random.fold_in(stream_key, 6), dim), (parts,), jnp.float32, least / len(cuts), high / len(cuts))
        return jnp.repeat(jnp.exp(draws), extent[dim] // parts).reshape((-1,) + (1,) * (len(extent) - dim - 1))

    gain = one(*cuts[0])
    for cut in cuts[1:]:
        gain = gain * one(*cut)
    return gain


def noise(own_key, extent, width, reach, shards=(), kind=jnp.bfloat16):
    values = width * jax.random.normal(own_key, extent, jnp.float32)
    if shards:
        values = values * block_levels(own_key, extent, shards, -0.22, 0.18)
    return jnp.clip(values, -reach, reach).astype(kind)


def setup_inputs(seed: int = 0) -> dict:
    splits = jax.random.split(jax.random.key(seed), 5)
    slab = noise(splits[0], (ROWS, COLS), 1.0, 6.0, ((0, 64), (1, 16)), jnp.float32)
    panel = noise(splits[1], (ROWS, NB), NB ** -0.5, 0.25, ((0, 64), (1, 16)), jnp.float32)
    tri_inverse = draw_tri_inverse(jax.random.fold_in(splits[4], 71), 0)
    pivots = draw_pivots(jax.random.fold_in(splits[4], 71), 0)
    return {"slab": slab, "panel": panel, "tri_inverse": tri_inverse, "pivots": pivots}


def reference(slab, panel, tri_inverse, pivots):
    leading = slab[:NB]
    rows_u = slab[pivots]
    swapped = slab.at[pivots].set(leading)
    u_block = jnp.dot(tri_inverse, rows_u, precision=lax.Precision.HIGHEST, preferred_element_type=jnp.float32)
    product = jnp.dot(panel, u_block, precision=lax.Precision.HIGHEST, preferred_element_type=jnp.float32)
    updated = swapped - product
    return updated.at[:NB].set(u_block)
```

```python
import functools

import jax
import jax.numpy as jnp
from jax import lax
from jax.experimental import pallas as pl
from jax.experimental.pallas import tpu as pltpu
from jax.sharding import PartitionSpec as P

NX, NY, NZ = 4, 8, 16
NB = 512
SLOTS = 10
BLK = SLOTS * 4
ZB = NX * BLK
NQ = NX * NZ * SLOTS
MESH = pl.DeviceIdType.MESH
F32, BF16 = jnp.float32, jnp.bfloat16


def split(v):
    hi = v.astype(BF16)
    return hi, (v - hi.astype(F32)).astype(BF16)


def dot(a, b):
    return jnp.dot(a, b, preferred_element_type=F32)


def iota(shape, dim):
    return lax.broadcasted_iota(jnp.int32, shape, dim)


def kernel(
    slab_hbm, panel_hbm, tri_hbm, piv_hbm, out_ref,
    slab, pivs, tri, rbuf, scp, scm, lx, lead, pt, thi, tlo, ahi, alo, onehot, selt, acc, got,
    in_sem, xs, xr, zps, zpr, zms, zmr, sps, spr, sms, smr, ls, lr, yps, ypr, yms, ymr, cs, cr,
):
    d = lax.axis_index("prow")
    p = lax.axis_index("pcol")
    z, x = d // NX, d % NX
    y, core = p // 2, p % 2

    def at_zx(zz, xx):
        return {"prow": lax.rem(zz + NZ, NZ) * NX + lax.rem(xx + NX, NX), "pcol": p}

    def at_y(yy, cc):
        return {"prow": d, "pcol": lax.rem(yy + NY, NY) * 2 + cc}

    x_to = {1: at_zx(z, x - 1), 2: at_zx(z, x + 2), 3: at_zx(z, x + 1)}
    up, down = at_zx(z + 1, x), at_zx(z - 1, x)
    y_up, y_down, other = at_y(y + 1, core), at_y(y - 1, core), at_y(y, 1 - core)

    def remote(src, dst, send, recv, dev):
        return pltpu.make_async_remote_copy(
            src_ref=src, dst_ref=dst, send_sem=send, recv_sem=recv, device_id=dev, device_id_type=MESH
        )

    c_slab = pltpu.make_async_copy(slab_hbm, slab, in_sem.at[0])
    c_panel = pltpu.make_async_copy(panel_hbm, pt.at[p], in_sem.at[1])
    c_tri = pltpu.make_async_copy(tri_hbm, tri, in_sem.at[2])
    c_piv = pltpu.make_async_copy(piv_hbm, pivs, in_sem.at[3])
    c_piv.start()
    c_slab.start()
    c_panel.start()
    c_tri.start()

    barrier = pltpu.get_barrier_semaphore()
    partners = [x_to[1], x_to[2], x_to[3], up, down, y_up, y_down, other]
    for dev in partners:
        pl.semaphore_signal(barrier, inc=1, device_id=dev, device_id_type=MESH)

    c_piv.wait()
    piv = pivs[...]
    own = lax.shift_right_logical(piv, 9)
    pivf = piv.astype(F32)
    basef = (own * NB).astype(F32)
    colp = jnp.transpose(jnp.broadcast_to(pivf, (128, NB)))
    ranks = []
    for c in range(4):
        sl = slice(c * 128, (c + 1) * 128)
        before = (colp < pivf[:, sl]) & (colp >= basef[:, sl])
        ranks.append(jnp.sum(jnp.where(before, 1.0, 0.0), axis=0, keepdims=True))
    rank = jnp.concatenate(ranks, axis=1).astype(jnp.int32)
    mine = own == d
    lrow = piv - d * NB

    c_slab.wait()
    for k in range(SLOTS):
        row = jnp.sum(jnp.where(mine & (rank == k), lrow, 0))
        picked = slab[pl.ds(row, 1), :]
        for c in range(4):
            rbuf[pl.ds(k * 4 + c, 1), :] = picked[:, c * 128 : (c + 1) * 128]

    pos = own * SLOTS + rank
    c_panel.wait()

    pl.semaphore_wait(barrier, len(partners))

    def zrows(slot, e):
        return rbuf.at[pl.ds(slot * ZB + e * BLK, BLK), :]

    sends = []

    def go(copy):
        copy.start()
        sends.append(copy)
        return copy

    x_in = {}
    for e in (3, 1, 2):
        x_in[e] = go(remote(zrows(0, 0), zrows(0, e), xs.at[e - 1], xr.at[e - 1], x_to[e]))

    def pslot(s):
        return 0 if s == 0 else 2 * s - 1

    def mslot(s):
        return 2 * s

    zp, zm = {}, {}

    def z_send(s, e, plus=True, minus=True):
        if plus:
            zp[s, e] = go(remote(zrows(pslot(s - 1), e), zrows(pslot(s), e), zps.at[s - 1, e], zpr.at[s - 1, e], up))
        if minus:
            zm[s, e] = go(remote(zrows(mslot(s - 1), e), zrows(mslot(s) if s < 8 else 15, e),
                                 zms.at[s - 1, e], zmr.at[s - 1, e], down))

    z_send(1, 0)

    def lead_rows(xd):
        rho = iota((NZ * SLOTS, 1), 0)
        i = lax.shift_right_logical(rho * 103, 10)
        half = lax.shift_right_logical(i, 1)
        zz = jnp.where((i & 1) == 1, (9 + half) & 15, 8 - half)
        want = (zz * NX + xd) * SLOTS + (rho - i * SLOTS)
        pick = jnp.where(pos == want, 1.0, 0.0).astype(BF16)
        hi, lo = split(slab[...])
        return dot(pick, hi) + dot(pick, lo)

    @pl.when(d == 0)
    def _():
        for xd in (1, 3, 2, 0):
            rows = lead_rows(xd)
            for c in range(4):
                part = rows[:, c * 128 : (c + 1) * 128]
                if xd:
                    lead[xd - 1, pl.ds(c, NZ * SLOTS, stride=4), :] = part
                else:
                    lx[pl.ds(c, NZ * SLOTS, stride=4), :] = part

    def yblock(yy):
        return pt.at[lax.rem(yy + NY, NY) * 2 + core]

    yp, ym, yc = {}, {}, {}

    def y_send(s):
        if s <= 4:
            b = yblock(y - (s - 1))
            yp[s] = go(remote(b, b, yps.at[s - 1], ypr.at[s - 1], y_up))
        if s <= 3:
            b = yblock(y + (s - 1))
            ym[s] = go(remote(b, b, yms.at[s - 1], ymr.at[s - 1], y_down))

    def c_send(i, yy):
        b = yblock(yy)
        yc[i] = go(remote(b, b, cs.at[i], cr.at[i], other))

    y_send(1)
    c_send(0, y)

    def lx_copy(ch, xd):
        rows = pl.ds(ch * 4 * BLK, 4 * BLK)
        return remote(lead.at[xd - 1, rows, :], lx.at[rows, :], ls.at[ch, xd - 1], lr.at[ch], at_zx(z, xd))

    @pl.when(d == 0)
    def _():
        for ch in range(4):
            for xd in (2, 1, 3):
                lx_copy(ch, xd).start()

    def lx_wait(ch):
        @pl.when((z == 0) & (x != 0))
        def _():
            lx_copy(ch, 1).wait_recv()

    sp, sm = {}, {}

    def sc_send(s):
        if s % 2 == 1:
            lx_wait((s - 1) // 2)
        own_p = remote(lx.at[pl.ds(2 * (s - 1) * BLK, BLK), :], scp.at[s - 1], sps.at[s - 1], spr.at[s - 1], up)
        sp[s] = remote(scp.at[max(s - 2, 0)], scp.at[s - 1], sps.at[s - 1], spr.at[s - 1], up)
        if s <= 7:
            own_m = remote(lx.at[pl.ds((2 * s - 1) * BLK, BLK), :], scm.at[s - 1], sms.at[s - 1], smr.at[s - 1], down)
            sm[s] = remote(scm.at[max(s - 2, 0)], scm.at[s - 1], sms.at[s - 1], smr.at[s - 1], down)

        @pl.when(z == 0)
        def _():
            own_p.start()
            if s <= 7:
                own_m.start()

        @pl.when((z >= 1) & (z <= s - 1) & (z <= 7))
        def _():
            sp[s].start()

        if s <= 7:
            @pl.when((z >= NZ - (s - 1)) & (z >= 10))
            def _():
                sm[s].start()

    def has_p(s):
        return (z >= 1) & (z <= s) & (z <= 8)

    def has_m(s):
        return (z >= NZ - s) & (z >= 9)

    def sc_wait(s):
        @pl.when(has_p(s))
        def _():
            sp[s].wait_recv()

        if s <= 7:
            @pl.when(has_m(s))
            def _():
                sm[s].wait_recv()

    def build_onehot():
        colpos = jnp.transpose(jnp.broadcast_to(pos.astype(F32), (128, NB)))
        for c in range(NQ // 128):
            q = iota((1, 128), 1) + c * 128
            slot = lax.shift_right_logical(q * 1639, 16)
            r = q - slot * 40
            e = lax.shift_right_logical(r * 103, 10)
            half = lax.shift_right_logical(slot + 1, 1)
            zz = (z + jnp.where((slot & 1) == 1, NZ - half, half)) & 15
            want = ((zz * NX + ((x + e) & 3)) * SLOTS + (r - e * SLOTS)).astype(F32)
            onehot[:, c * 128 : (c + 1) * 128] = jnp.where(colpos == want, 1.0, 0.0).astype(BF16)

    def tri_tile(t):
        rows = slice(t * 128, (t + 1) * 128)
        hi, lo = split(tri[rows, :])
        thi[rows, :] = dot(hi, onehot[...]).astype(BF16)
        tlo[rows, :] = dot(lo, onehot[...]).astype(BF16)

    def start_acc():
        k = iota((128, 1), 0)
        at = jnp.sum(jnp.where(mine & (rank == k), lrow + 1, 0), axis=1, keepdims=True) - 1
        hit = jnp.where(at == iota((128, NB), 1), 1.0, 0.0)
        sel = jnp.transpose(hit)
        selt[...] = sel.astype(BF16)
        keep = 1.0 - jnp.sum(sel, axis=1, keepdims=True)
        keep = jnp.where(d == 0, 0.0, keep)
        acc[...] = slab[...] * keep

    def w_tile(t):
        cols = slice(t * 128, (t + 1) * 128)
        mat = jnp.transpose(pt[:, :, cols].reshape(NB, 128))
        hi, lo = split(mat)
        w = dot(hi, thi[...]) + (dot(hi, tlo[...]) + dot(lo, thi[...]))
        top = thi[cols, :].astype(F32) + tlo[cols, :].astype(F32)
        a_hi, a_lo = split(jnp.where(d == 0, top, -w))
        ahi[cols, :] = a_hi
        alo[cols, :] = a_lo

    def r_chunk(q0, n):
        v = jnp.concatenate([rbuf[pl.ds(q0 * 4 + c, n, stride=4), :] for c in range(4)], axis=1)
        return split(v)

    def gemm(q0):
        hi, lo = r_chunk(q0, 256)
        cols = slice(q0, q0 + 256)
        acc[...] += dot(ahi[:, cols], hi) + (dot(ahi[:, cols], lo) + dot(alo[:, cols], hi))

    for e in (3, 1, 2):
        x_in[e].wait_recv()
        z_send(1, e)
    sc_send(1)
    c_tri.wait()
    build_onehot()
    tri_tile(0)

    for s in range(2, 9):
        for e in (0, 3, 1, 2):
            zp[s - 1, e].wait_recv()
            if s < 8 or e in (0, 1):
                z_send(s, e, minus=False)
            zm[s - 1, e].wait_recv()
            if s < 8 or e in (2, 3):
                z_send(s, e, plus=False)
        if 2 <= s <= 5:
            yp[s - 1].wait_recv()
            if s - 1 <= 3:
                ym[s - 1].wait_recv()
            y_send(s)
            c_send(s - 1, y - (s - 1))
            if s - 1 <= 3:
                c_send(s + 3, y + (s - 1))
        sc_wait(s - 1)
        sc_send(s)
        if s == 2:
            tri_tile(1)
            tri_tile(2)
        elif s == 3:
            tri_tile(3)
        elif s == 4:
            start_acc()
        elif s == 6:
            for i in range(8):
                yc[i].wait_recv()
            w_tile(0)
            w_tile(1)
        elif s == 7:
            w_tile(2)
            w_tile(3)
            gemm(0)
        elif s == 8:
            gemm(256)

    for e in (0, 1):
        zp[8, e].wait_recv()
    for e in (2, 3):
        zm[8, e].wait_recv()
    sc_wait(8)

    @pl.when(z == 0)
    def _():
        got[...] = lx[pl.ds(15 * BLK, BLK), :]

    @pl.when((z >= 1) & (z <= 8))
    def _():
        got[...] = scp[7]

    @pl.when(z >= 9)
    def _():
        got[...] = scm[6]

    place = jnp.concatenate([got[pl.ds(c, SLOTS, stride=4), :] for c in range(4)], axis=1)
    place = jnp.concatenate([place, jnp.zeros((128 - SLOTS, NB), F32)], axis=0)
    place = jnp.where(d == 0, 0.0, place)
    r_hi, r_lo = r_chunk(512, 128)
    p_hi, p_lo = split(place)
    r_hi = jnp.concatenate([r_hi, p_hi], axis=0)
    r_lo = jnp.concatenate([r_lo, p_lo], axis=0)
    for t in range(4):
        rows = slice(t * 128, (t + 1) * 128)
        left = jnp.concatenate([ahi[rows, 512:], selt[rows, :]], axis=1)
        low = alo[rows, 512:]
        out_ref[rows, :] = acc[rows, :] + (dot(left, r_hi) + (dot(left, r_lo) + dot(low, r_hi[:128])))

    for copy in sends:
        copy.wait_send()

    @pl.when(d == 0)
    def _():
        for ch in range(4):
            for xd in (2, 1, 3):
                lx_copy(ch, xd).wait_send()

    for s in range(1, 9):
        @pl.when((z == 0) | ((z >= 1) & (z <= s - 1) & (z <= 7)))
        def _(s=s):
            sp[s].wait_send()

        if s <= 7:
            @pl.when((z == 0) | ((z >= NZ - (s - 1)) & (z >= 10)))
            def _(s=s):
                sm[s].wait_send()


def per_device(slab, panel, tri_inverse, pivots):
    dma = pltpu.SemaphoreType.DMA
    vm = pltpu.VMEM
    hbm = pl.BlockSpec(memory_space=pltpu.HBM)
    return pl.pallas_call(
        kernel,
        out_shape=jax.ShapeDtypeStruct((NB, NB), F32),
        in_specs=[hbm] * 4,
        out_specs=pl.BlockSpec(memory_space=pltpu.VMEM),
        scratch_shapes=[
            vm((NB, NB), F32), vm((1, NB), jnp.int32), vm((NB, NB), F32),
            vm((NZ * ZB, 128), F32), vm((8, BLK, 128), F32), vm((7, BLK, 128), F32),
            vm((NZ * BLK, 128), F32), vm((3, NZ * BLK, 128), F32), vm((16, 32, NB), F32),
            vm((NB, NQ), BF16), vm((NB, NQ), BF16), vm((NB, NQ), BF16), vm((NB, NQ), BF16),
            vm((NB, NQ), BF16), vm((NB, 128), BF16), vm((NB, NB), F32), vm((BLK, 128), F32),
            dma((4,)), dma((3,)), dma((3,)),
            dma((8, 4)), dma((8, 4)), dma((8, 4)), dma((8, 4)),
            dma((8,)), dma((8,)), dma((7,)), dma((7,)), dma((4, 3)), dma((4,)),
            dma((4,)), dma((4,)), dma((3,)), dma((3,)), dma((8,)), dma((8,)),
        ],
        compiler_params=pltpu.CompilerParams(
            collective_id=0, has_side_effects=True, vmem_limit_bytes=32 * 1024 * 1024
        ),
    )(slab, panel.T, tri_inverse, pivots.reshape(1, NB))


def solution(mesh):
    return jax.shard_map(
        per_device,
        mesh=mesh,
        in_specs=(P("prow", "pcol"), P("prow", "pcol"), P(), P()),
        out_specs=P("prow", "pcol"),
        check_vma=False,
    )
```

```python
import functools

import jax
import jax.numpy as jnp
from jax import lax
from jax.experimental import pallas as pl
from jax.experimental.pallas import tpu as pltpu
from jax.sharding import PartitionSpec as P

NX, NY, NZ = 4, 8, 16
NB = 512
SLOTS = 10
BLK = SLOTS * 4
ZB = NX * BLK
NQ = NX * NZ * SLOTS
MESH = pl.DeviceIdType.MESH
F32, BF16 = jnp.float32, jnp.bfloat16
STEPS = (1, -1, 2, -2, 3, 5, -5)
OFFSETS = (0, -1, 1, -2, 2, -5, 5, -4, 4, -6, 6, -3, 3, -7, 7, -8)
DIRECT = (0, 13, 14, 15)
LAG = 3


def split(v):
    hi = v.astype(BF16)
    return hi, (v - hi.astype(F32)).astype(BF16)


def dot(a, b):
    return jnp.dot(a, b, preferred_element_type=F32)


def iota(shape, dim):
    return lax.broadcasted_iota(jnp.int32, shape, dim)


def pivot_ranks(piv, own):
    pivf = piv.astype(F32)
    basef = (own * NB).astype(F32)
    colp = jnp.transpose(jnp.broadcast_to(pivf, (128, NB)))
    ranks = []
    for c in range(4):
        sl = slice(c * 128, (c + 1) * 128)
        before = (colp < pivf[:, sl]) & (colp >= basef[:, sl])
        ranks.append(jnp.sum(jnp.where(before, 1.0, 0.0), axis=0, keepdims=True))
    return jnp.concatenate(ranks, axis=1).astype(jnp.int32)


def lead_kernel(slab_hbm, piv_hbm, lx_hbm, slab, pivs, lead, in_sem, ls, lr):
    d = lax.axis_index("prow")
    p = lax.axis_index("pcol")
    barrier = pltpu.get_barrier_semaphore()

    def to_x(xd):
        return pltpu.make_async_remote_copy(
            src_ref=lead.at[xd], dst_ref=lx_hbm, send_sem=ls.at[xd], recv_sem=lr,
            device_id={"prow": xd, "pcol": p}, device_id_type=MESH,
        )

    @pl.when((d >= 1) & (d < NX))
    def _():
        pl.semaphore_signal(barrier, inc=1, device_id={"prow": 0, "pcol": p}, device_id_type=MESH)

    @pl.when(d == 0)
    def _():
        c_piv = pltpu.make_async_copy(piv_hbm, pivs, in_sem.at[0])
        c_slab = pltpu.make_async_copy(slab_hbm, slab, in_sem.at[1])
        c_piv.start()
        c_slab.start()
        c_piv.wait()
        piv = pivs[...]
        own = lax.shift_right_logical(piv, 9)
        pos = own * SLOTS + pivot_ranks(piv, own)
        c_slab.wait()
        hi, lo = split(slab[...])
        for xd in range(NX):
            rho = iota((NZ * SLOTS, 1), 0)
            i = lax.shift_right_logical(rho * 103, 10)
            want = (i * NX + xd) * SLOTS + (rho - i * SLOTS)
            pick = jnp.where(pos == want, 1.0, 0.0).astype(BF16)
            rows = dot(pick, hi) + dot(pick, lo)
            for c in range(4):
                lead[xd, pl.ds(c, NZ * SLOTS, stride=4), :] = rows[:, c * 128 : (c + 1) * 128]
        pl.semaphore_wait(barrier, NX - 1)
        for xd in (2, 1, 3):
            to_x(xd).start()
        mine = pltpu.make_async_copy(lead.at[0], lx_hbm, in_sem.at[0])
        mine.start()
        mine.wait()
        for xd in (2, 1, 3):
            to_x(xd).wait_send()

    @pl.when((d >= 1) & (d < NX))
    def _():
        to_x(1).wait_recv()


def kernel(
    slab_hbm, panel_hbm, tri_hbm, piv_hbm, lx, out_ref,
    slab, pivs, tri, rbuf, pt, thi, tlo, ahi, alo, onehot, selt, acc, got,
    in_sem, zs, zr, xs, xr, gs, gr, ys, yr, cs, cr,
):
    d = lax.axis_index("prow")
    p = lax.axis_index("pcol")
    z, x = d // NX, d % NX
    y, core = p // 2, p % 2

    def at_zx(zz, xx):
        return {"prow": lax.rem(zz + NZ, NZ) * NX + lax.rem(xx + NX, NX), "pcol": p}

    def at_y(yy, cc):
        return {"prow": d, "pcol": lax.rem(yy + NY, NY) * 2 + cc}

    x_to = {1: at_zx(z, x - 1), 2: at_zx(z, x + 2), 3: at_zx(z, x + 1)}
    other = at_y(y, 1 - core)

    def remote(src, dst, send, recv, dev):
        return pltpu.make_async_remote_copy(
            src_ref=src, dst_ref=dst, send_sem=send, recv_sem=recv, device_id=dev, device_id_type=MESH
        )

    c_slab = pltpu.make_async_copy(slab_hbm, slab, in_sem.at[0])
    c_panel = pltpu.make_async_copy(panel_hbm, pt.at[p], in_sem.at[1])
    c_tri = pltpu.make_async_copy(tri_hbm, tri, in_sem.at[2])
    c_piv = pltpu.make_async_copy(piv_hbm, pivs, in_sem.at[3])
    c_piv.start()
    c_slab.start()
    c_panel.start()
    c_tri.start()

    barrier = pltpu.get_barrier_semaphore()
    partners = [at_zx(z - o, x) for o in STEPS] + [x_to[1], x_to[2], x_to[3], other]
    partners += [at_y(y + o, core) for o in (1, -1, 2, -2)]
    for dev in partners:
        pl.semaphore_signal(barrier, inc=1, device_id=dev, device_id_type=MESH)
    far = z != 0
    for o in STEPS:
        far = far & (z != o % NZ)

    @pl.when(far)
    def _():
        pl.semaphore_signal(barrier, inc=1, device_id=at_zx(0, x), device_id_type=MESH)

    c_piv.wait()
    piv = pivs[...]
    own = lax.shift_right_logical(piv, 9)
    rank = pivot_ranks(piv, own)
    mine = own == d
    lrow = piv - d * NB

    c_slab.wait()
    for k in range(SLOTS):
        row = jnp.sum(jnp.where(mine & (rank == k), lrow, 0))
        picked = slab[pl.ds(row, 1), :]
        for c in range(4):
            rbuf[pl.ds(k * 4 + c, 1), :] = picked[:, c * 128 : (c + 1) * 128]

    pos = own * SLOTS + rank

    c_panel.wait()
    pl.semaphore_wait(barrier, len(partners) + jnp.where(z == 0, NZ - 1 - len(STEPS), 0))

    def zrows(slot, e):
        return rbuf.at[pl.ds(slot * ZB + e * BLK, BLK), :]

    sends = []

    def go(copy):
        copy.start()
        sends.append(copy)
        return copy

    z_in = {}

    def z_send(o_from, step):
        o = (o_from - step + 8) % NZ - 8
        slot = OFFSETS.index(o)
        z_in[slot] = go(remote(zrows(OFFSETS.index(o_from), 0), zrows(slot, 0), zs.at[slot], zr.at[slot], at_zx(z + step, x)))

    for step in (5, -5, 1, -1, 2, -2):
        z_send(0, step)

    x_in = {}

    def x_send(slot, e, e_from=0):
        x_in[slot, e] = go(remote(zrows(slot, e_from), zrows(slot, e), xs.at[slot, e - 1], xr.at[slot, e - 1],
                                  x_to[{0: e, 1: 1, 3: 3}[e_from]]))

    def x_first(slot):
        x_send(slot, 1)
        x_send(slot, 3)
        if slot in DIRECT:
            x_send(slot, 2)

    def x_second(slot):
        x_in[slot, 1].wait_recv()
        x_in[slot, 3].wait_recv()
        if slot not in DIRECT:
            x_send(slot, 2, 1 if slot % 2 == 0 else 3)

    x_first(0)

    def yblock(yy, cc=core):
        return pt.at[lax.rem(yy + NY, NY) * 2 + cc]

    y_in, c_in = {}, {}
    half = 16

    def y_send(i, yy, step, rows=None):
        ref = yblock(yy) if rows is None else yblock(yy).at[pl.ds(rows, half), :]
        y_in[i] = go(remote(ref, ref, ys.at[i], yr.at[i], at_y(y + step, core)))

    def c_send(i, yy):
        c_in[i] = go(remote(yblock(yy), yblock(yy), cs.at[i], cr.at[i], other))

    for i, step in enumerate((2, -2, 1, -1)):
        y_send(i, y, step)
    c_send(7, y)

    def lx_out(zz):
        return remote(lx.at[pl.ds(zz * BLK, BLK), :], got, gs.at[zz - 1], gr, at_zx(zz, x))

    @pl.when(z == 0)
    def _():
        for zz in range(1, NZ):
            lx_out((zz * 7) % NZ).start()

    def build_onehot():
        colpos = jnp.transpose(jnp.broadcast_to(pos.astype(F32), (128, NB)))
        for c in range(NQ // 128):
            q = iota((1, 128), 1) + c * 128
            slot = lax.shift_right_logical(q * 1639, 16)
            r = q - slot * 40
            e = lax.shift_right_logical(r * 103, 10)
            off = jnp.zeros_like(q)
            for n, o in enumerate(OFFSETS):
                off = jnp.where(slot == n, o + NZ, off)
            zz = (z + off) & 15
            want = ((zz * NX + ((x + e) & 3)) * SLOTS + (r - e * SLOTS)).astype(F32)
            onehot[:, c * 128 : (c + 1) * 128] = jnp.where(colpos == want, 1.0, 0.0).astype(BF16)

    def tri_tile(t):
        rows = slice(t * 256, (t + 1) * 256)
        hi, lo = split(tri[rows, :])
        thi[rows, :] = dot(hi, onehot[...]).astype(BF16)
        tlo[rows, :] = dot(lo, onehot[...]).astype(BF16)

    def start_acc():
        k = iota((128, 1), 0)
        at = jnp.sum(jnp.where(mine & (rank == k), lrow + 1, 0), axis=1, keepdims=True) - 1
        hit = jnp.where(at == iota((128, NB), 1), 1.0, 0.0)
        sel = jnp.transpose(hit)
        selt[...] = sel.astype(BF16)
        keep = 1.0 - jnp.sum(sel, axis=1, keepdims=True)
        keep = jnp.where(d == 0, 0.0, keep)
        acc[...] = slab[...] * keep

    def w_tile(t):
        cols = slice(t * 256, (t + 1) * 256)
        mat = jnp.transpose(pt[:, :, cols].reshape(NB, 256))
        hi, lo = split(mat)
        w = dot(hi, thi[...]) + (dot(hi, tlo[...]) + dot(lo, thi[...]))
        top = thi[cols, :].astype(F32) + tlo[cols, :].astype(F32)
        a_hi, a_lo = split(jnp.where(d == 0, top, -w))
        ahi[cols, :] = a_hi
        alo[cols, :] = a_lo

    def r_chunk(q0, n):
        v = jnp.concatenate([rbuf[pl.ds(q0 * 4 + c, n, stride=4), :] for c in range(4)], axis=1)
        return split(v)

    def gemm(q0):
        hi, lo = r_chunk(q0, 256)
        cols = slice(q0, q0 + 256)
        acc[...] += dot(ahi[:, cols], hi) + (dot(ahi[:, cols], lo) + dot(alo[:, cols], hi))

    def y_first(i, o):
        y_in[i].wait_recv()
        if o == -2:
            y_send(4, y - 2, 1)
            y_send(6, y - 2, 2, 0)
        if o == 2:
            y_send(5, y + 2, -1)
            y_send(7, y + 2, -2, half)
        c_send(i, y + o)

    c_tri.wait()
    build_onehot()
    tri_tile(0)
    for n in range(1, NZ):
        z_in[n].wait_recv()
        if OFFSETS[n] == -5:
            for step in (3, 2, -2, 1, -1):
                z_send(-5, step)
        if OFFSETS[n] == 5:
            for step in (-2, 2, -1, 1):
                z_send(5, step)
        x_first(n)
        if n > LAG:
            x_second(n - LAG)
        if n == 2:
            tri_tile(1)
        if n == 4:
            y_first(0, -2)
            y_first(1, 2)
        if n == 6:
            start_acc()
            y_first(2, -1)
            y_first(3, 1)
        if n == 10:
            y_first(4, -3)
            y_first(5, 3)
        if n == 12:
            y_in[6].wait_recv()
            y_in[7].wait_recv()
            c_send(6, y + 4)
    x_second(0)
    for n in range(NZ - LAG, NZ):
        x_second(n)
    for i in range(8):
        c_in[i].wait_recv()
    w_tile(0)
    w_tile(1)
    for slot in range(7):
        x_in[slot, 2].wait_recv()
    gemm(0)
    for slot in range(7, 13):
        x_in[slot, 2].wait_recv()
    gemm(256)
    for slot in range(13, 16):
        x_in[slot, 2].wait_recv()

    c_own = pltpu.make_async_copy(lx.at[pl.ds(0, BLK), :], got, in_sem.at[0])

    @pl.when(z == 0)
    def _():
        c_own.start()
        c_own.wait()

    @pl.when(z != 0)
    def _():
        lx_out(1).wait_recv()

    place = jnp.concatenate([got[pl.ds(c, SLOTS, stride=4), :] for c in range(4)], axis=1)
    place = jnp.concatenate([place, jnp.zeros((128 - SLOTS, NB), F32)], axis=0)
    place = jnp.where(d == 0, 0.0, place)
    r_hi, r_lo = r_chunk(512, 128)
    p_hi, p_lo = split(place)
    r_hi = jnp.concatenate([r_hi, p_hi], axis=0)
    r_lo = jnp.concatenate([r_lo, p_lo], axis=0)
    for t in range(4):
        rows = slice(t * 128, (t + 1) * 128)
        left = jnp.concatenate([ahi[rows, 512:], selt[rows, :]], axis=1)
        low = alo[rows, 512:]
        out_ref[rows, :] = acc[rows, :] + (dot(left, r_hi) + (dot(left, r_lo) + dot(low, r_hi[:128])))

    for copy in sends:
        copy.wait_send()

    @pl.when(z == 0)
    def _():
        for zz in range(1, NZ):
            lx_out(zz).wait_send()


def per_device(slab, panel, tri_inverse, pivots):
    dma = pltpu.SemaphoreType.DMA
    vm = pltpu.VMEM
    hbm = pl.BlockSpec(memory_space=pltpu.HBM)
    pivots = pivots.reshape(1, NB)
    lx = pl.pallas_call(
        lead_kernel,
        out_shape=jax.ShapeDtypeStruct((NZ * BLK, 128), F32),
        in_specs=[hbm] * 2,
        out_specs=hbm,
        scratch_shapes=[
            vm((NB, NB), F32), vm((1, NB), jnp.int32), vm((NX, NZ * BLK, 128), F32), dma((2,)), dma((NX,)), dma,
        ],
        compiler_params=pltpu.CompilerParams(
            collective_id=1, has_side_effects=True, vmem_limit_bytes=63_000_000
        ),
    )(slab, pivots)
    return pl.pallas_call(
        kernel,
        out_shape=jax.ShapeDtypeStruct((NB, NB), F32),
        in_specs=[hbm] * 5,
        out_specs=pl.BlockSpec(memory_space=pltpu.VMEM),
        scratch_shapes=[
            vm((NB, NB), F32), vm((1, NB), jnp.int32), vm((NB, NB), F32),
            vm((NZ * ZB, 128), F32), vm((16, 32, NB), F32),
            vm((NB, NQ), BF16), vm((NB, NQ), BF16), vm((NB, NQ), BF16), vm((NB, NQ), BF16),
            vm((NB, NQ), BF16), vm((NB, 128), BF16), vm((NB, NB), F32), vm((BLK, 128), F32),
            dma((4,)), dma((16,)), dma((16,)), dma((16, 3)), dma((16, 3)),
            dma((15,)), dma, dma((8,)), dma((8,)), dma((8,)), dma((8,)),
        ],
        compiler_params=pltpu.CompilerParams(
            collective_id=0, has_side_effects=True, vmem_limit_bytes=63_000_000
        ),
    )(slab, panel.T, tri_inverse, pivots, lx)


def solution(mesh):
    return jax.shard_map(
        per_device,
        mesh=mesh,
        in_specs=(P("prow", "pcol"), P("prow", "pcol"), P(), P()),
        out_specs=P("prow", "pcol"),
        check_vma=False,
    )
```

```python
import functools

import jax
import jax.numpy as jnp
from jax import lax
from jax.experimental import pallas as pl
from jax.experimental.pallas import tpu as pltpu
from jax.sharding import PartitionSpec as P

NX, NY, NZ = 4, 8, 16
NB = 512
SLOTS = 10
BLK = SLOTS * 4
ZB = NX * BLK
NQ = NX * NZ * SLOTS
MESH = pl.DeviceIdType.MESH
F32, BF16 = jnp.float32, jnp.bfloat16
STEPS = (1, -1, 2, -2, 3, -3, 4, -4)
OFFSETS = (0, -1, 1, -2, 2, -4, 4, -3, 3, -5, 5, -6, 6, -7, 7, -8)
DIRECT = (0,)
LAG = 6


def split(v):
    hi = v.astype(BF16)
    return hi, (v - hi.astype(F32)).astype(BF16)


def dot(a, b):
    return jnp.dot(a, b, preferred_element_type=F32)


def iota(shape, dim):
    return lax.broadcasted_iota(jnp.int32, shape, dim)


def pivot_ranks(piv, own):
    pivf = piv.astype(F32)
    basef = (own * NB).astype(F32)
    colp = jnp.transpose(jnp.broadcast_to(pivf, (128, NB)))
    ranks = []
    for c in range(4):
        sl = slice(c * 128, (c + 1) * 128)
        before = (colp < pivf[:, sl]) & (colp >= basef[:, sl])
        ranks.append(jnp.sum(jnp.where(before, 1.0, 0.0), axis=0, keepdims=True))
    return jnp.concatenate(ranks, axis=1).astype(jnp.int32)


def lead_kernel(slab_hbm, piv_hbm, lx_hbm, slab, pivs, lead, in_sem, ls, lr):
    d = lax.axis_index("prow")
    p = lax.axis_index("pcol")
    barrier = pltpu.get_barrier_semaphore()

    def to_x(xd):
        return pltpu.make_async_remote_copy(
            src_ref=lead.at[xd], dst_ref=lx_hbm, send_sem=ls.at[xd], recv_sem=lr,
            device_id={"prow": xd, "pcol": p}, device_id_type=MESH,
        )

    @pl.when((d >= 1) & (d < NX))
    def _():
        pl.semaphore_signal(barrier, inc=1, device_id={"prow": 0, "pcol": p}, device_id_type=MESH)

    @pl.when(d == 0)
    def _():
        c_piv = pltpu.make_async_copy(piv_hbm, pivs, in_sem.at[0])
        c_slab = pltpu.make_async_copy(slab_hbm, slab, in_sem.at[1])
        c_piv.start()
        c_slab.start()
        c_piv.wait()
        piv = pivs[...]
        own = lax.shift_right_logical(piv, 9)
        pos = own * SLOTS + pivot_ranks(piv, own)
        c_slab.wait()
        hi, lo = split(slab[...])
        for xd in range(NX):
            rho = iota((NZ * SLOTS, 1), 0)
            i = lax.shift_right_logical(rho * 103, 10)
            want = (i * NX + xd) * SLOTS + (rho - i * SLOTS)
            pick = jnp.where(pos == want, 1.0, 0.0).astype(BF16)
            rows = dot(pick, hi) + dot(pick, lo)
            for c in range(4):
                lead[xd, pl.ds(c, NZ * SLOTS, stride=4), :] = rows[:, c * 128 : (c + 1) * 128]
        pl.semaphore_wait(barrier, NX - 1)
        for xd in (2, 1, 3):
            to_x(xd).start()
        mine = pltpu.make_async_copy(lead.at[0], lx_hbm, in_sem.at[0])
        mine.start()
        mine.wait()
        for xd in (2, 1, 3):
            to_x(xd).wait_send()

    @pl.when((d >= 1) & (d < NX))
    def _():
        to_x(1).wait_recv()


def kernel(
    slab_hbm, panel_hbm, tri_hbm, piv_hbm, lx, out_ref,
    slab, pivs, tri, rbuf, pt, thi, tlo, ahi, alo, onehot, selt, acc, got,
    in_sem, zs, zr, xs, xr, gs, gr, ys, yr, cs, cr,
):
    d = lax.axis_index("prow")
    p = lax.axis_index("pcol")
    z, x = d // NX, d % NX
    y, core = p // 2, p % 2

    def at_zx(zz, xx):
        return {"prow": lax.rem(zz + NZ, NZ) * NX + lax.rem(xx + NX, NX), "pcol": p}

    def at_y(yy, cc):
        return {"prow": d, "pcol": lax.rem(yy + NY, NY) * 2 + cc}

    x_to = {1: at_zx(z, x - 1), 2: at_zx(z, x + 2), 3: at_zx(z, x + 1)}
    other = at_y(y, 1 - core)

    def remote(src, dst, send, recv, dev):
        return pltpu.make_async_remote_copy(
            src_ref=src, dst_ref=dst, send_sem=send, recv_sem=recv, device_id=dev, device_id_type=MESH
        )

    c_slab = pltpu.make_async_copy(slab_hbm, slab, in_sem.at[0])
    c_panel = pltpu.make_async_copy(panel_hbm, pt.at[p], in_sem.at[1])
    c_tri = pltpu.make_async_copy(tri_hbm, tri, in_sem.at[2])
    c_piv = pltpu.make_async_copy(piv_hbm, pivs, in_sem.at[3])
    c_piv.start()
    c_slab.start()
    c_panel.start()
    c_tri.start()

    barrier = pltpu.get_barrier_semaphore()
    partners = [at_zx(z - o, x) for o in STEPS] + [x_to[1], x_to[2], x_to[3], other]
    partners += [at_y(y + o, core) for o in (1, -1, 2, -2)]
    for dev in partners:
        pl.semaphore_signal(barrier, inc=1, device_id=dev, device_id_type=MESH)
    far = z != 0
    for o in STEPS:
        far = far & (z != o % NZ)

    @pl.when(far)
    def _():
        pl.semaphore_signal(barrier, inc=1, device_id=at_zx(0, x), device_id_type=MESH)

    c_piv.wait()
    piv = pivs[...]
    own = lax.shift_right_logical(piv, 9)
    rank = pivot_ranks(piv, own)
    mine = own == d
    lrow = piv - d * NB

    c_slab.wait()
    for k in range(SLOTS):
        row = jnp.sum(jnp.where(mine & (rank == k), lrow, 0))
        picked = slab[pl.ds(row, 1), :]
        for c in range(4):
            rbuf[pl.ds(k * 4 + c, 1), :] = picked[:, c * 128 : (c + 1) * 128]

    pos = own * SLOTS + rank

    c_panel.wait()
    pl.semaphore_wait(barrier, len(partners) + jnp.where(z == 0, NZ - 1 - len(STEPS), 0))

    def zrows(slot, e):
        return rbuf.at[pl.ds(slot * ZB + e * BLK, BLK), :]

    sends = []

    def go(copy):
        copy.start()
        sends.append(copy)
        return copy

    z_in = {}

    def z_send(o_from, step):
        o = (o_from - step + 8) % NZ - 8
        slot = OFFSETS.index(o)
        z_in[slot] = go(remote(zrows(OFFSETS.index(o_from), 0), zrows(slot, 0), zs.at[slot], zr.at[slot], at_zx(z + step, x)))

    for step in (4, -4, 1, -1, 2, -2, 3, -3):
        z_send(0, step)

    x_in = {}

    def x_send(slot, e, e_from=0):
        x_in[slot, e] = go(remote(zrows(slot, e_from), zrows(slot, e), xs.at[slot, e - 1], xr.at[slot, e - 1],
                                  x_to[{0: e, 1: 1, 3: 3}[e_from]]))

    def x_first(slot):
        x_send(slot, 1)
        x_send(slot, 3)
        if slot in DIRECT:
            x_send(slot, 2)

    def x_second(slot):
        x_in[slot, 1].wait_recv()
        x_in[slot, 3].wait_recv()
        if slot not in DIRECT:
            x_send(slot, 2, 1 if slot % 2 == 0 else 3)

    x_first(0)

    def yblock(yy, cc=core):
        return pt.at[lax.rem(yy + NY, NY) * 2 + cc]

    y_in, c_in = {}, {}
    half = 16

    def y_send(i, yy, step, rows=None):
        ref = yblock(yy) if rows is None else yblock(yy).at[pl.ds(rows, half), :]
        y_in[i] = go(remote(ref, ref, ys.at[i], yr.at[i], at_y(y + step, core)))

    def c_send(i, yy):
        c_in[i] = go(remote(yblock(yy), yblock(yy), cs.at[i], cr.at[i], other))

    for i, step in enumerate((2, -2, 1, -1)):
        y_send(i, y, step)
    c_send(7, y)

    def lx_out(zz):
        return remote(lx.at[pl.ds(zz * BLK, BLK), :], got, gs.at[zz - 1], gr, at_zx(zz, x))

    @pl.when(z == 0)
    def _():
        for zz in range(1, NZ):
            lx_out((zz * 7) % NZ).start()

    def build_onehot():
        colpos = jnp.transpose(jnp.broadcast_to(pos.astype(F32), (128, NB)))
        for c in range(NQ // 128):
            q = iota((1, 128), 1) + c * 128
            slot = lax.shift_right_logical(q * 1639, 16)
            r = q - slot * 40
            e = lax.shift_right_logical(r * 103, 10)
            off = jnp.zeros_like(q)
            for n, o in enumerate(OFFSETS):
                off = jnp.where(slot == n, o + NZ, off)
            zz = (z + off) & 15
            want = ((zz * NX + ((x + e) & 3)) * SLOTS + (r - e * SLOTS)).astype(F32)
            onehot[:, c * 128 : (c + 1) * 128] = jnp.where(colpos == want, 1.0, 0.0).astype(BF16)

    def tri_tile(t):
        rows = slice(t * 256, (t + 1) * 256)
        hi, lo = split(tri[rows, :])
        thi[rows, :] = dot(hi, onehot[...]).astype(BF16)
        tlo[rows, :] = dot(lo, onehot[...]).astype(BF16)

    def start_acc():
        k = iota((128, 1), 0)
        at = jnp.sum(jnp.where(mine & (rank == k), lrow + 1, 0), axis=1, keepdims=True) - 1
        hit = jnp.where(at == iota((128, NB), 1), 1.0, 0.0)
        sel = jnp.transpose(hit)
        selt[...] = sel.astype(BF16)
        keep = 1.0 - jnp.sum(sel, axis=1, keepdims=True)
        keep = jnp.where(d == 0, 0.0, keep)
        acc[...] = slab[...] * keep

    def w_tile(t):
        cols = slice(t * 256, (t + 1) * 256)
        mat = jnp.transpose(pt[:, :, cols].reshape(NB, 256))
        hi, lo = split(mat)
        w = dot(hi, thi[...]) + (dot(hi, tlo[...]) + dot(lo, thi[...]))
        top = thi[cols, :].astype(F32) + tlo[cols, :].astype(F32)
        a_hi, a_lo = split(jnp.where(d == 0, top, -w))
        ahi[cols, :] = a_hi
        alo[cols, :] = a_lo

    def r_chunk(q0, n):
        v = jnp.concatenate([rbuf[pl.ds(q0 * 4 + c, n, stride=4), :] for c in range(4)], axis=1)
        return split(v)

    def gemm(q0):
        hi, lo = r_chunk(q0, 256)
        cols = slice(q0, q0 + 256)
        acc[...] += dot(ahi[:, cols], hi) + (dot(ahi[:, cols], lo) + dot(alo[:, cols], hi))

    def y_first(i, o):
        y_in[i].wait_recv()
        if o == -2:
            y_send(4, y - 2, 1)
            y_send(6, y - 2, 2, 0)
        if o == 2:
            y_send(5, y + 2, -1)
            y_send(7, y + 2, -2, half)
        c_send(i, y + o)

    c_tri.wait()
    build_onehot()
    tri_tile(0)
    for n in range(1, NZ):
        z_in[n].wait_recv()
        if OFFSETS[n] == -4:
            for step in (1, 4, 2, 3):
                z_send(-4, step)
        if OFFSETS[n] == 4:
            for step in (-1, -2, -3):
                z_send(4, step)
        x_first(n)
        if n > LAG:
            x_second(n - LAG)
        if n == 2:
            tri_tile(1)
        if n == 4:
            y_first(0, -2)
            y_first(1, 2)
        if n == 8:
            start_acc()
            y_first(2, -1)
            y_first(3, 1)
        if n == 11:
            y_first(4, -3)
            y_first(5, 3)
        if n == 13:
            y_in[6].wait_recv()
            y_in[7].wait_recv()
            c_send(6, y + 4)
    x_second(0)
    for n in range(NZ - LAG, NZ):
        x_second(n)
    for i in range(8):
        c_in[i].wait_recv()
    w_tile(0)
    w_tile(1)
    for slot in range(7):
        x_in[slot, 2].wait_recv()
    gemm(0)
    for slot in range(7, 13):
        x_in[slot, 2].wait_recv()
    gemm(256)
    for slot in range(13, 16):
        x_in[slot, 2].wait_recv()

    c_own = pltpu.make_async_copy(lx.at[pl.ds(0, BLK), :], got, in_sem.at[0])

    @pl.when(z == 0)
    def _():
        c_own.start()
        c_own.wait()

    @pl.when(z != 0)
    def _():
        lx_out(1).wait_recv()

    place = jnp.concatenate([got[pl.ds(c, SLOTS, stride=4), :] for c in range(4)], axis=1)
    place = jnp.concatenate([place, jnp.zeros((128 - SLOTS, NB), F32)], axis=0)
    place = jnp.where(d == 0, 0.0, place)
    r_hi, r_lo = r_chunk(512, 128)
    p_hi, p_lo = split(place)
    r_hi = jnp.concatenate([r_hi, p_hi], axis=0)
    r_lo = jnp.concatenate([r_lo, p_lo], axis=0)
    for t in range(4):
        rows = slice(t * 128, (t + 1) * 128)
        left = jnp.concatenate([ahi[rows, 512:], selt[rows, :]], axis=1)
        low = alo[rows, 512:]
        out_ref[rows, :] = acc[rows, :] + (dot(left, r_hi) + (dot(left, r_lo) + dot(low, r_hi[:128])))

    for copy in sends:
        copy.wait_send()

    @pl.when(z == 0)
    def _():
        for zz in range(1, NZ):
            lx_out(zz).wait_send()


def per_device(slab, panel, tri_inverse, pivots):
    dma = pltpu.SemaphoreType.DMA
    vm = pltpu.VMEM
    hbm = pl.BlockSpec(memory_space=pltpu.HBM)
    pivots = pivots.reshape(1, NB)
    lx = pl.pallas_call(
        lead_kernel,
        out_shape=jax.ShapeDtypeStruct((NZ * BLK, 128), F32),
        in_specs=[hbm] * 2,
        out_specs=hbm,
        scratch_shapes=[
            vm((NB, NB), F32), vm((1, NB), jnp.int32), vm((NX, NZ * BLK, 128), F32), dma((2,)), dma((NX,)), dma,
        ],
        compiler_params=pltpu.CompilerParams(
            collective_id=1, has_side_effects=True, vmem_limit_bytes=63_000_000
        ),
    )(slab, pivots)
    return pl.pallas_call(
        kernel,
        out_shape=jax.ShapeDtypeStruct((NB, NB), F32),
        in_specs=[hbm] * 5,
        out_specs=pl.BlockSpec(memory_space=pltpu.VMEM),
        scratch_shapes=[
            vm((NB, NB), F32), vm((1, NB), jnp.int32), vm((NB, NB), F32),
            vm((NZ * ZB, 128), F32), vm((16, 32, NB), F32),
            vm((NB, NQ), BF16), vm((NB, NQ), BF16), vm((NB, NQ), BF16), vm((NB, NQ), BF16),
            vm((NB, NQ), BF16), vm((NB, 128), BF16), vm((NB, NB), F32), vm((BLK, 128), F32),
            dma((4,)), dma((16,)), dma((16,)), dma((16, 3)), dma((16, 3)),
            dma((15,)), dma, dma((8,)), dma((8,)), dma((8,)), dma((8,)),
        ],
        compiler_params=pltpu.CompilerParams(
            collective_id=0, has_side_effects=True, vmem_limit_bytes=63_000_000
        ),
    )(slab, panel.T, tri_inverse, pivots, lx)


def solution(mesh):
    return jax.shard_map(
        per_device,
        mesh=mesh,
        in_specs=(P("prow", "pcol"), P("prow", "pcol"), P(), P()),
        out_specs=P("prow", "pcol"),
        check_vma=False,
    )
```

```python
import functools

import jax
import jax.numpy as jnp
from jax import lax
from jax.experimental import pallas as pl
from jax.experimental.pallas import tpu as pltpu
from jax.sharding import PartitionSpec as P

NX, NY, NZ = 4, 8, 16
NB = 512
SLOTS = 10
BLK = SLOTS * 4
ZB = NX * BLK
NQ = NX * NZ * SLOTS
MESH = pl.DeviceIdType.MESH
F32, BF16 = jnp.float32, jnp.bfloat16
STEPS = (1, -1, 2, -2, 3, -3, 4, -4)
OFFSETS = (0, -1, 1, -2, 2, -4, 4, -3, 3, -5, 5, -6, 6, -7, 7, -8)
NEAR = (1, 2)
LAG = 6


def split(v):
    hi = v.astype(BF16)
    return hi, (v - hi.astype(F32)).astype(BF16)


def dot(a, b):
    return jnp.dot(a, b, preferred_element_type=F32)


def iota(shape, dim):
    return lax.broadcasted_iota(jnp.int32, shape, dim)


def pivot_ranks(piv, own):
    pivf = piv.astype(F32)
    basef = (own * NB).astype(F32)
    colp = jnp.transpose(jnp.broadcast_to(pivf, (128, NB)))
    ranks = []
    for c in range(4):
        sl = slice(c * 128, (c + 1) * 128)
        before = (colp < pivf[:, sl]) & (colp >= basef[:, sl])
        ranks.append(jnp.sum(jnp.where(before, 1.0, 0.0), axis=0, keepdims=True))
    return jnp.concatenate(ranks, axis=1).astype(jnp.int32)


def lead_kernel(slab_hbm, piv_hbm, lx_hbm, slab, pivs, lead, in_sem, ls, lr):
    d = lax.axis_index("prow")
    p = lax.axis_index("pcol")
    barrier = pltpu.get_barrier_semaphore()

    def to_x(xd):
        return pltpu.make_async_remote_copy(
            src_ref=lead.at[xd], dst_ref=lx_hbm.at[pl.ds(0, NZ * BLK), :], send_sem=ls.at[xd], recv_sem=lr,
            device_id={"prow": xd, "pcol": p}, device_id_type=MESH,
        )

    @pl.when((d >= 1) & (d < NX))
    def _():
        pl.semaphore_signal(barrier, inc=1, device_id={"prow": 0, "pcol": p}, device_id_type=MESH)

    @pl.when(d == 0)
    def _():
        c_piv = pltpu.make_async_copy(piv_hbm, pivs, in_sem.at[0])
        c_slab = pltpu.make_async_copy(slab_hbm, slab, in_sem.at[1])
        c_piv.start()
        c_slab.start()
        c_piv.wait()
        piv = pivs[...]
        own = lax.shift_right_logical(piv, 9)
        pos = own * SLOTS + pivot_ranks(piv, own)
        c_slab.wait()
        hi, lo = split(slab[...])
        for xd in range(NX):
            rho = iota((NZ * SLOTS, 1), 0)
            i = lax.shift_right_logical(rho * 103, 10)
            want = (i * NX + xd) * SLOTS + (rho - i * SLOTS)
            pick = jnp.where(pos == want, 1.0, 0.0).astype(BF16)
            rows = dot(pick, hi) + dot(pick, lo)
            for c in range(4):
                lead[xd, pl.ds(c, NZ * SLOTS, stride=4), :] = rows[:, c * 128 : (c + 1) * 128]
        pl.semaphore_wait(barrier, NX - 1)
        for xd in (2, 1, 3):
            to_x(xd).start()
        mine = pltpu.make_async_copy(lead.at[0], lx_hbm.at[pl.ds(0, NZ * BLK), :], in_sem.at[0])
        mine.start()
        mine.wait()
        for xd in (2, 1, 3):
            to_x(xd).wait_send()

    @pl.when((d >= 1) & (d < NX))
    def _():
        to_x(1).wait_recv()


def kernel(
    slab_hbm, panel_hbm, tri_hbm, piv_hbm, lx, out_ref,
    slab, pivs, tri, rbuf, pt, thi, tlo, ahi, alo, onehot, selt, acc, got,
    in_sem, zs, zr, xs, xr, gs, gr, ys, yr, cs, cr,
):
    d = lax.axis_index("prow")
    p = lax.axis_index("pcol")
    z, x = d // NX, d % NX
    y, core = p // 2, p % 2

    def at_zx(zz, xx):
        return {"prow": lax.rem(zz + NZ, NZ) * NX + lax.rem(xx + NX, NX), "pcol": p}

    def at_y(yy, cc):
        return {"prow": d, "pcol": lax.rem(yy + NY, NY) * 2 + cc}

    x_to = {1: at_zx(z, x - 1), 2: at_zx(z, x + 2), 3: at_zx(z, x + 1)}
    other = at_y(y, 1 - core)

    def remote(src, dst, send, recv, dev):
        return pltpu.make_async_remote_copy(
            src_ref=src, dst_ref=dst, send_sem=send, recv_sem=recv, device_id=dev, device_id_type=MESH
        )

    c_slab = pltpu.make_async_copy(slab_hbm, slab, in_sem.at[0])
    c_panel = pltpu.make_async_copy(panel_hbm, pt.at[p], in_sem.at[1])
    c_tri = pltpu.make_async_copy(tri_hbm, tri, in_sem.at[2])
    c_piv = pltpu.make_async_copy(piv_hbm, pivs, in_sem.at[3])
    c_piv.start()
    c_slab.start()
    c_panel.start()
    c_tri.start()

    barrier = pltpu.get_barrier_semaphore()
    partners = [at_zx(z - o, x) for o in STEPS] + [x_to[1], x_to[2], x_to[3], other]
    partners += [at_y(y + o, core) for o in (1, -1, 2, -2)]
    for dev in partners:
        pl.semaphore_signal(barrier, inc=1, device_id=dev, device_id_type=MESH)
    far = z != 0
    for o in STEPS:
        far = far & (z != o % NZ)

    @pl.when(far)
    def _():
        pl.semaphore_signal(barrier, inc=1, device_id=at_zx(0, x), device_id_type=MESH)

    c_piv.wait()
    piv = pivs[...]
    own = lax.shift_right_logical(piv, 9)
    rank = pivot_ranks(piv, own)
    mine = own == d
    lrow = piv - d * NB

    c_slab.wait()
    for k in range(SLOTS):
        row = jnp.sum(jnp.where(mine & (rank == k), lrow, 0))
        picked = slab[pl.ds(row, 1), :]
        for c in range(4):
            rbuf[pl.ds(k * 4 + c, 1), :] = picked[:, c * 128 : (c + 1) * 128]

    pos = own * SLOTS + rank

    c_panel.wait()
    pl.semaphore_wait(barrier, len(partners) + jnp.where(z == 0, NZ - 1 - len(STEPS), 0))

    def zrows(slot, e):
        return rbuf.at[pl.ds(slot * ZB + e * BLK, BLK), :]

    sends = []

    def go(copy):
        copy.start()
        sends.append(copy)
        return copy

    z_in = {}

    def z_send(o_from, step):
        o = (o_from - step + 8) % NZ - 8
        slot = OFFSETS.index(o)
        z_in[slot] = go(remote(zrows(OFFSETS.index(o_from), 0), zrows(slot, 0), zs.at[slot], zr.at[slot], at_zx(z + step, x)))

    for step in (4, -4, 1, -1, 2, -2, 3, -3):
        z_send(0, step)

    x_in = {}

    def x_send(slot, e, e_from=0):
        x_in[slot, e] = go(remote(zrows(slot, e_from), zrows(slot, e), xs.at[slot, e - 1], xr.at[slot, e - 1],
                                  x_to[{0: e, 1: 1, 3: 3}[e_from]]))

    def x_first(slot):
        x_send(slot, 1)
        x_send(slot, 3)
        if slot == 0:
            x_send(slot, 2)

    def x_second(slot):
        x_in[slot, 1].wait_recv()
        x_in[slot, 3].wait_recv()
        if slot not in NEAR:
            x_send(slot, 2, 1 if slot % 2 == 0 else 3)

    def near_send(e):
        x_in[0, e].wait_recv()
        for slot in NEAR:
            x_in[slot, e] = go(remote(zrows(0, e), zrows(slot, e), xs.at[slot, e - 1], xr.at[slot, e - 1],
                                      at_zx(z - OFFSETS[slot], x)))

    x_first(0)

    def yblock(yy, cc=core):
        return pt.at[lax.rem(yy + NY, NY) * 2 + cc]

    y_in, c_in = {}, {}
    half = 16

    def y_send(i, yy, step, rows=None):
        ref = yblock(yy) if rows is None else yblock(yy).at[pl.ds(rows, half), :]
        y_in[i] = go(remote(ref, ref, ys.at[i], yr.at[i], at_y(y + step, core)))

    def c_send(i, yy):
        c_in[i] = go(remote(yblock(yy), yblock(yy), cs.at[i], cr.at[i], other))

    for i, step in enumerate((2, -2, 1, -1)):
        y_send(i, y, step)
    c_send(7, y)

    def lx_out(zz):
        return remote(lx.at[pl.ds(zz * BLK, BLK), :], got, gs.at[zz - 1], gr, at_zx(zz, x))

    @pl.when(z == 0)
    def _():
        for zz in range(1, NZ):
            lx_out((zz * 7) % NZ).start()

    def build_onehot():
        colpos = jnp.transpose(jnp.broadcast_to(pos.astype(F32), (128, NB)))
        for c in range(NQ // 128):
            q = iota((1, 128), 1) + c * 128
            slot = lax.shift_right_logical(q * 1639, 16)
            r = q - slot * 40
            e = lax.shift_right_logical(r * 103, 10)
            off = jnp.zeros_like(q)
            for n, o in enumerate(OFFSETS):
                off = jnp.where(slot == n, o + NZ, off)
            zz = (z + off) & 15
            want = ((zz * NX + ((x + e) & 3)) * SLOTS + (r - e * SLOTS)).astype(F32)
            onehot[:, c * 128 : (c + 1) * 128] = jnp.where(colpos == want, 1.0, 0.0).astype(BF16)

    def tri_tile(t):
        rows = slice(t * 256, (t + 1) * 256)
        hi, lo = split(tri[rows, :])
        thi[rows, :] = dot(hi, onehot[...]).astype(BF16)
        tlo[rows, :] = dot(lo, onehot[...]).astype(BF16)

    def start_acc():
        k = iota((128, 1), 0)
        at = jnp.sum(jnp.where(mine & (rank == k), lrow + 1, 0), axis=1, keepdims=True) - 1
        hit = jnp.where(at == iota((128, NB), 1), 1.0, 0.0)
        sel = jnp.transpose(hit)
        selt[...] = sel.astype(BF16)
        keep = 1.0 - jnp.sum(sel, axis=1, keepdims=True)
        keep = jnp.where(d == 0, 0.0, keep)
        acc[...] = slab[...] * keep

    def w_tile(t):
        cols = slice(t * 256, (t + 1) * 256)
        mat = jnp.transpose(pt[:, :, cols].reshape(NB, 256))
        hi, lo = split(mat)
        w = dot(hi, thi[...]) + (dot(hi, tlo[...]) + dot(lo, thi[...]))
        top = thi[cols, :].astype(F32) + tlo[cols, :].astype(F32)
        a_hi, a_lo = split(jnp.where(d == 0, top, -w))
        ahi[cols, :] = a_hi
        alo[cols, :] = a_lo

    def r_chunk(q0, n):
        v = jnp.concatenate([rbuf[pl.ds(q0 * 4 + c, n, stride=4), :] for c in range(4)], axis=1)
        return split(v)

    def gemm(q0):
        hi, lo = r_chunk(q0, 256)
        cols = slice(q0, q0 + 256)
        acc[...] += dot(ahi[:, cols], hi) + (dot(ahi[:, cols], lo) + dot(alo[:, cols], hi))

    def y_first(i, o):
        y_in[i].wait_recv()
        if o == -2:
            y_send(4, y - 2, 1)
            y_send(6, y - 2, 2, 0)
        if o == 2:
            y_send(5, y + 2, -1)
            y_send(7, y + 2, -2, half)
        c_send(i, y + o)

    c_tri.wait()
    build_onehot()
    tri_tile(0)
    for n in range(1, NZ):
        z_in[n].wait_recv()
        if OFFSETS[n] == -4:
            for step in (1, 4, 2, 3):
                z_send(-4, step)
        if OFFSETS[n] == 4:
            for step in (-1, -2, -3):
                z_send(4, step)
        if n not in NEAR:
            x_first(n)
        if n == 4:
            for e in (3, 1, 2):
                near_send(e)
        if n > LAG:
            x_second(n - LAG)
        if n == 2:
            tri_tile(1)
        if n == 4:
            y_first(0, -2)
            y_first(1, 2)
        if n == 8:
            start_acc()
            y_first(2, -1)
            y_first(3, 1)
        if n == 11:
            y_first(4, -3)
            y_first(5, 3)
        if n == 13:
            y_in[6].wait_recv()
            y_in[7].wait_recv()
            c_send(6, y + 4)
    for n in range(NZ - LAG, NZ):
        x_second(n)
        if n == 11:
            for i in range(8):
                c_in[i].wait_recv()
            w_tile(0)
        if n == 13:
            w_tile(1)
    for slot in range(1, 7):
        x_in[slot, 2].wait_recv()
    gemm(0)
    for slot in range(7, 13):
        x_in[slot, 2].wait_recv()
    gemm(256)
    for slot in range(13, 16):
        x_in[slot, 2].wait_recv()

    c_own = pltpu.make_async_copy(lx.at[pl.ds(0, BLK), :], got, in_sem.at[0])

    @pl.when(z == 0)
    def _():
        c_own.start()
        c_own.wait()

    @pl.when(z != 0)
    def _():
        lx_out(1).wait_recv()

    place = jnp.concatenate([got[pl.ds(c, SLOTS, stride=4), :] for c in range(4)], axis=1)
    place = jnp.concatenate([place, jnp.zeros((128 - SLOTS, NB), F32)], axis=0)
    place = jnp.where(d == 0, 0.0, place)
    r_hi, r_lo = r_chunk(512, 128)
    p_hi, p_lo = split(place)
    r_hi = jnp.concatenate([r_hi, p_hi], axis=0)
    r_lo = jnp.concatenate([r_lo, p_lo], axis=0)
    for t in range(4):
        rows = slice(t * 128, (t + 1) * 128)
        left = jnp.concatenate([ahi[rows, 512:], selt[rows, :]], axis=1)
        low = alo[rows, 512:]
        out_ref[rows, :] = acc[rows, :] + (dot(left, r_hi) + (dot(left, r_lo) + dot(low, r_hi[:128])))

    for copy in sends:
        copy.wait_send()

    @pl.when(z == 0)
    def _():
        for zz in range(1, NZ):
            lx_out(zz).wait_send()


def per_device(slab, panel, tri_inverse, pivots):
    dma = pltpu.SemaphoreType.DMA
    vm = pltpu.VMEM
    hbm = pl.BlockSpec(memory_space=pltpu.HBM)
    pivots = pivots.reshape(1, NB)
    lx = pl.pallas_call(
        lead_kernel,
        out_shape=jax.ShapeDtypeStruct((8 * NZ * BLK, 128), F32),
        in_specs=[hbm] * 2,
        out_specs=hbm,
        scratch_shapes=[
            vm((NB, NB), F32), vm((1, NB), jnp.int32), vm((NX, NZ * BLK, 128), F32), dma((2,)), dma((NX,)), dma,
        ],
        compiler_params=pltpu.CompilerParams(
            collective_id=1, has_side_effects=True, vmem_limit_bytes=63_000_000
        ),
    )(slab, pivots)
    return pl.pallas_call(
        kernel,
        out_shape=jax.ShapeDtypeStruct((NB, NB), F32),
        in_specs=[hbm] * 5,
        out_specs=pl.BlockSpec(memory_space=pltpu.VMEM),
        scratch_shapes=[
            vm((NB, NB), F32), vm((1, NB), jnp.int32), vm((NB, NB), F32),
            vm((NZ * ZB, 128), F32), vm((16, 32, NB), F32),
            vm((NB, NQ), BF16), vm((NB, NQ), BF16), vm((NB, NQ), BF16), vm((NB, NQ), BF16),
            vm((NB, NQ), BF16), vm((NB, 128), BF16), vm((NB, NB), F32), vm((BLK, 128), F32),
            dma((4,)), dma((16,)), dma((16,)), dma((16, 3)), dma((16, 3)),
            dma((15,)), dma, dma((8,)), dma((8,)), dma((8,)), dma((8,)),
        ],
        compiler_params=pltpu.CompilerParams(
            collective_id=0, has_side_effects=True, vmem_limit_bytes=55_000_000
        ),
    )(slab, panel.T, tri_inverse, pivots, lx)


def solution(mesh):
    return jax.shard_map(
        per_device,
        mesh=mesh,
        in_specs=(P("prow", "pcol"), P("prow", "pcol"), P(), P()),
        out_specs=P("prow", "pcol"),
        check_vma=False,
    )
```

```python
import functools

import jax
import jax.numpy as jnp
from jax import lax
from jax.experimental import pallas as pl
from jax.experimental.pallas import tpu as pltpu
from jax.sharding import PartitionSpec as P

NX, NY, NZ = 4, 8, 16
NB = 512
SLOTS = 10
BLK = SLOTS * 4
ZB = NX * BLK
NQ = NX * NZ * SLOTS
MESH = pl.DeviceIdType.MESH
F32, BF16 = jnp.float32, jnp.bfloat16
STEPS = (1, -1, 2, -2, 3, -3, 4, -4)
OFFSETS = (0, -1, 1, -2, 2, -4, 4, -3, 3, -5, 5, -6, 6, -7, 7, -8)
LAG = 6


def split(v):
    hi = v.astype(BF16)
    return hi, (v - hi.astype(F32)).astype(BF16)


def dot(a, b):
    return jnp.dot(a, b, preferred_element_type=F32)


def iota(shape, dim):
    return lax.broadcasted_iota(jnp.int32, shape, dim)


def pivot_ranks(piv, own):
    pivf = piv.astype(F32)
    basef = (own * NB).astype(F32)
    colp = jnp.transpose(jnp.broadcast_to(pivf, (128, NB)))
    ranks = []
    for c in range(4):
        sl = slice(c * 128, (c + 1) * 128)
        before = (colp < pivf[:, sl]) & (colp >= basef[:, sl])
        ranks.append(jnp.sum(jnp.where(before, 1.0, 0.0), axis=0, keepdims=True))
    return jnp.concatenate(ranks, axis=1).astype(jnp.int32)


def lead_kernel(slab_hbm, piv_hbm, lx_hbm, slab, pivs, lead, in_sem, ls, lr):
    d = lax.axis_index("prow")
    p = lax.axis_index("pcol")
    barrier = pltpu.get_barrier_semaphore()

    def to_x(xd):
        return pltpu.make_async_remote_copy(
            src_ref=lead.at[xd], dst_ref=lx_hbm.at[pl.ds(0, NZ * BLK), :], send_sem=ls.at[xd], recv_sem=lr,
            device_id={"prow": xd, "pcol": p}, device_id_type=MESH,
        )

    @pl.when((d >= 1) & (d < NX))
    def _():
        pl.semaphore_signal(barrier, inc=1, device_id={"prow": 0, "pcol": p}, device_id_type=MESH)

    @pl.when(d == 0)
    def _():
        c_piv = pltpu.make_async_copy(piv_hbm, pivs, in_sem.at[0])
        c_slab = pltpu.make_async_copy(slab_hbm, slab, in_sem.at[1])
        c_piv.start()
        c_slab.start()
        c_piv.wait()
        piv = pivs[...]
        own = lax.shift_right_logical(piv, 9)
        pos = own * SLOTS + pivot_ranks(piv, own)
        c_slab.wait()
        hi, lo = split(slab[...])
        for xd in range(NX):
            rho = iota((NZ * SLOTS, 1), 0)
            i = lax.shift_right_logical(rho * 103, 10)
            want = (i * NX + xd) * SLOTS + (rho - i * SLOTS)
            pick = jnp.where(pos == want, 1.0, 0.0).astype(BF16)
            rows = dot(pick, hi) + dot(pick, lo)
            for c in range(4):
                lead[xd, pl.ds(c, NZ * SLOTS, stride=4), :] = rows[:, c * 128 : (c + 1) * 128]
        pl.semaphore_wait(barrier, NX - 1)
        for xd in (2, 1, 3):
            to_x(xd).start()
        mine = pltpu.make_async_copy(lead.at[0], lx_hbm.at[pl.ds(0, NZ * BLK), :], in_sem.at[0])
        mine.start()
        mine.wait()
        for xd in (2, 1, 3):
            to_x(xd).wait_send()

    @pl.when((d >= 1) & (d < NX))
    def _():
        to_x(1).wait_recv()


def kernel(
    slab_hbm, panel_hbm, tri_hbm, piv_hbm, lx, out_ref,
    slab, pivs, tri, rbuf, pt, thi, tlo, ahi, alo, onehot, selt, acc, got,
    in_sem, zs, zr, xs, xr, gs, gr, ys, yr, cs, cr,
):
    d = lax.axis_index("prow")
    p = lax.axis_index("pcol")
    z, x = d // NX, d % NX
    y, core = p // 2, p % 2

    def at_zx(zz, xx):
        return {"prow": lax.rem(zz + NZ, NZ) * NX + lax.rem(xx + NX, NX), "pcol": p}

    def at_y(yy, cc):
        return {"prow": d, "pcol": lax.rem(yy + NY, NY) * 2 + cc}

    x_to = {1: at_zx(z, x - 1), 2: at_zx(z, x + 2), 3: at_zx(z, x + 1)}
    other = at_y(y, 1 - core)

    def remote(src, dst, send, recv, dev):
        return pltpu.make_async_remote_copy(
            src_ref=src, dst_ref=dst, send_sem=send, recv_sem=recv, device_id=dev, device_id_type=MESH
        )

    c_slab = pltpu.make_async_copy(slab_hbm, slab, in_sem.at[0])
    c_panel = pltpu.make_async_copy(panel_hbm, pt.at[p], in_sem.at[1])
    c_tri = pltpu.make_async_copy(tri_hbm, tri, in_sem.at[2])
    c_piv = pltpu.make_async_copy(piv_hbm, pivs, in_sem.at[3])
    c_piv.start()
    c_slab.start()
    c_panel.start()

    barrier = pltpu.get_barrier_semaphore()
    partners = [at_zx(z - o, x) for o in STEPS] + [x_to[1], x_to[2], x_to[3], other]
    partners += [at_y(y + o, core) for o in (1, -1, 2, -2)]
    for dev in partners:
        pl.semaphore_signal(barrier, inc=1, device_id=dev, device_id_type=MESH)
    far = z != 0
    for o in STEPS:
        far = far & (z != o % NZ)

    @pl.when(far)
    def _():
        pl.semaphore_signal(barrier, inc=1, device_id=at_zx(0, x), device_id_type=MESH)

    c_piv.wait()
    piv = pivs[...]
    own = lax.shift_right_logical(piv, 9)
    rank = pivot_ranks(piv, own)
    mine = own == d
    lrow = piv - d * NB

    c_slab.wait()
    for k in range(SLOTS):
        row = jnp.sum(jnp.where(mine & (rank == k), lrow, 0))
        picked = slab[pl.ds(row, 1), :]
        for c in range(4):
            rbuf[pl.ds(k * 4 + c, 1), :] = picked[:, c * 128 : (c + 1) * 128]

    pos = own * SLOTS + rank

    c_tri.start()
    c_panel.wait()
    pl.semaphore_wait(barrier, len(partners) + jnp.where(z == 0, NZ - 1 - len(STEPS), 0))

    def zrows(slot, e):
        return rbuf.at[pl.ds(slot * ZB + e * BLK, BLK), :]

    sends = []

    def go(copy):
        copy.start()
        sends.append(copy)
        return copy

    z_in = {}

    def z_send(o_from, step):
        o = (o_from - step + 8) % NZ - 8
        slot = OFFSETS.index(o)
        z_in[slot] = go(remote(zrows(OFFSETS.index(o_from), 0), zrows(slot, 0), zs.at[slot], zr.at[slot], at_zx(z + step, x)))

    for step in (4, -4, 1, -1, 2, -2, 3, -3):
        z_send(0, step)

    x_in = {}

    def x_send(slot, e, e_from=0):
        x_in[slot, e] = go(remote(zrows(slot, e_from), zrows(slot, e), xs.at[slot, e - 1], xr.at[slot, e - 1],
                                  x_to[{0: e, 1: 1, 3: 3}[e_from]]))

    def x_first(slot):
        x_send(slot, 1)
        x_send(slot, 3)
        if slot == 0:
            x_send(slot, 2)

    def x_second(slot):
        x_in[slot, 1].wait_recv()
        x_in[slot, 3].wait_recv()
        x_send(slot, 2, 1 if slot % 2 == 0 else 3)

    x_first(0)

    def yblock(yy, cc=core):
        return pt.at[lax.rem(yy + NY, NY) * 2 + cc]

    y_in, c_in = {}, {}
    half = 16

    def y_send(i, yy, step, rows=None):
        ref = yblock(yy) if rows is None else yblock(yy).at[pl.ds(rows, half), :]
        y_in[i] = go(remote(ref, ref, ys.at[i], yr.at[i], at_y(y + step, core)))

    def c_send(i, yy):
        c_in[i] = go(remote(yblock(yy), yblock(yy), cs.at[i], cr.at[i], other))

    for i, step in enumerate((2, -2, 1, -1)):
        y_send(i, y, step)
    c_send(7, y)

    def lx_out(zz):
        return remote(lx.at[pl.ds(zz * BLK, BLK), :], got, gs.at[zz - 1], gr, at_zx(zz, x))

    def build_onehot():
        colpos = jnp.transpose(jnp.broadcast_to(pos.astype(F32), (128, NB)))
        for c in range(NQ // 128):
            q = iota((1, 128), 1) + c * 128
            slot = lax.shift_right_logical(q * 1639, 16)
            r = q - slot * 40
            e = lax.shift_right_logical(r * 103, 10)
            off = jnp.zeros_like(q)
            for n, o in enumerate(OFFSETS):
                off = jnp.where(slot == n, o + NZ, off)
            zz = (z + off) & 15
            want = ((zz * NX + ((x + e) & 3)) * SLOTS + (r - e * SLOTS)).astype(F32)
            onehot[:, c * 128 : (c + 1) * 128] = jnp.where(colpos == want, 1.0, 0.0).astype(BF16)

    def tri_tile(t):
        rows = slice(t * 256, (t + 1) * 256)
        hi, lo = split(tri[rows, :])
        thi[rows, :] = dot(hi, onehot[...]).astype(BF16)
        tlo[rows, :] = dot(lo, onehot[...]).astype(BF16)

    def start_acc():
        k = iota((128, 1), 0)
        at = jnp.sum(jnp.where(mine & (rank == k), lrow + 1, 0), axis=1, keepdims=True) - 1
        hit = jnp.where(at == iota((128, NB), 1), 1.0, 0.0)
        sel = jnp.transpose(hit)
        selt[...] = sel.astype(BF16)
        keep = 1.0 - jnp.sum(sel, axis=1, keepdims=True)
        keep = jnp.where(d == 0, 0.0, keep)
        acc[...] = slab[...] * keep

    def w_tile(t):
        cols = slice(t * 256, (t + 1) * 256)
        mat = jnp.transpose(pt[:, :, cols].reshape(NB, 256))
        hi, lo = split(mat)
        w = dot(hi, thi[...]) + (dot(hi, tlo[...]) + dot(lo, thi[...]))
        top = thi[cols, :].astype(F32) + tlo[cols, :].astype(F32)
        a_hi, a_lo = split(jnp.where(d == 0, top, -w))
        ahi[cols, :] = a_hi
        alo[cols, :] = a_lo

    def r_chunk(q0, n):
        v = jnp.concatenate([rbuf[pl.ds(q0 * 4 + c, n, stride=4), :] for c in range(4)], axis=1)
        return split(v)

    def gemm(q0):
        hi, lo = r_chunk(q0, 256)
        cols = slice(q0, q0 + 256)
        acc[...] += dot(ahi[:, cols], hi) + (dot(ahi[:, cols], lo) + dot(alo[:, cols], hi))

    def y_first(i, o):
        y_in[i].wait_recv()
        if o == -2:
            y_send(4, y - 2, 1)
            y_send(6, y - 2, 2, 0)
        if o == 2:
            y_send(5, y + 2, -1)
            y_send(7, y + 2, -2, half)
        c_send(i, y + o)

    c_tri.wait()
    build_onehot()
    tri_tile(0)
    for n in range(1, NZ):
        z_in[n].wait_recv()
        if OFFSETS[n] == -4:
            for step in (1, 4, 2, 3):
                z_send(-4, step)
        if OFFSETS[n] == 4:
            for step in (-1, -2, -3):
                z_send(4, step)
        x_first(n)
        if n == 4:
            for e in (1, 3, 2):
                x_in[0, e].wait_recv()
        if n > LAG:
            x_second(n - LAG)
        if n == 2:
            tri_tile(1)
        if n == 4:
            y_first(0, -2)
            y_first(1, 2)
        if n == 7:
            @pl.when(z == 0)
            def _():
                for zz in range(1, NZ):
                    lx_out((zz * 7) % NZ).start()

        if n == 8:
            start_acc()
            y_first(2, -1)
            y_first(3, 1)
        if n == 11:
            y_first(4, -3)
            y_first(5, 3)
        if n == 13:
            y_in[6].wait_recv()
            y_in[7].wait_recv()
            c_send(6, y + 4)
    for n in range(NZ - LAG, NZ):
        x_second(n)
        if n == 11:
            for i in range(8):
                c_in[i].wait_recv()
            w_tile(0)
        if n == 13:
            w_tile(1)
    for slot in range(1, 7):
        x_in[slot, 2].wait_recv()
    gemm(0)
    for slot in range(7, 13):
        x_in[slot, 2].wait_recv()
    gemm(256)
    for slot in range(13, 16):
        x_in[slot, 2].wait_recv()

    c_own = pltpu.make_async_copy(lx.at[pl.ds(0, BLK), :], got, in_sem.at[0])

    @pl.when(z == 0)
    def _():
        c_own.start()
        c_own.wait()

    @pl.when(z != 0)
    def _():
        lx_out(1).wait_recv()

    place = jnp.concatenate([got[pl.ds(c, SLOTS, stride=4), :] for c in range(4)], axis=1)
    place = jnp.concatenate([place, jnp.zeros((128 - SLOTS, NB), F32)], axis=0)
    place = jnp.where(d == 0, 0.0, place)
    r_hi, r_lo = r_chunk(512, 128)
    p_hi, p_lo = split(place)
    r_hi = jnp.concatenate([r_hi, p_hi], axis=0)
    r_lo = jnp.concatenate([r_lo, p_lo], axis=0)
    for t in range(4):
        rows = slice(t * 128, (t + 1) * 128)
        left = jnp.concatenate([ahi[rows, 512:], selt[rows, :]], axis=1)
        low = alo[rows, 512:]
        out_ref[rows, :] = acc[rows, :] + (dot(left, r_hi) + (dot(left, r_lo) + dot(low, r_hi[:128])))

    for copy in sends:
        copy.wait_send()

    @pl.when(z == 0)
    def _():
        for zz in range(1, NZ):
            lx_out(zz).wait_send()


def per_device(slab, panel, tri_inverse, pivots):
    dma = pltpu.SemaphoreType.DMA
    vm = pltpu.VMEM
    hbm = pl.BlockSpec(memory_space=pltpu.HBM)
    pivots = pivots.reshape(1, NB)
    lx = pl.pallas_call(
        lead_kernel,
        out_shape=jax.ShapeDtypeStruct((8 * NZ * BLK, 128), F32),
        in_specs=[hbm] * 2,
        out_specs=hbm,
        scratch_shapes=[
            vm((NB, NB), F32), vm((1, NB), jnp.int32), vm((NX, NZ * BLK, 128), F32), dma((2,)), dma((NX,)), dma,
        ],
        compiler_params=pltpu.CompilerParams(
            collective_id=1, has_side_effects=True, vmem_limit_bytes=63_000_000
        ),
    )(slab, pivots)
    return pl.pallas_call(
        kernel,
        out_shape=jax.ShapeDtypeStruct((NB, NB), F32),
        in_specs=[hbm] * 5,
        out_specs=pl.BlockSpec(memory_space=pltpu.VMEM),
        scratch_shapes=[
            vm((NB, NB), F32), vm((1, NB), jnp.int32), vm((NB, NB), F32),
            vm((NZ * ZB, 128), F32), vm((16, 32, NB), F32),
            vm((NB, NQ), BF16), vm((NB, NQ), BF16), vm((NB, NQ), BF16), vm((NB, NQ), BF16),
            vm((NB, NQ), BF16), vm((NB, 128), BF16), vm((NB, NB), F32), vm((BLK, 128), F32),
            dma((4,)), dma((16,)), dma((16,)), dma((16, 3)), dma((16, 3)),
            dma((15,)), dma, dma((8,)), dma((8,)), dma((8,)), dma((8,)),
        ],
        compiler_params=pltpu.CompilerParams(
            collective_id=0, has_side_effects=True, vmem_limit_bytes=55_000_000
        ),
    )(slab, panel.T, tri_inverse, pivots, lx)


def solution(mesh):
    return jax.shard_map(
        per_device,
        mesh=mesh,
        in_specs=(P("prow", "pcol"), P("prow", "pcol"), P(), P()),
        out_specs=P("prow", "pcol"),
        check_vma=False,
    )
```
